768 devices in a mesh: dp: 64 (over z_hi, y, core), mp: 12 (over z_lo, x).
Axes of the slice: x: 4, y: 8, z: 12 (z_hi: 4, z_lo: 3; z = z_hi * 3 + z_lo), core: 2. Of those that a mesh axis runs over, the one named last changes fastest.
Arguments:
- queries: bfloat16 [1024, 6144], P('dp', 'mp'), may hold values from -160 to 160
- prefix_pool: bfloat16 [384, 6, 2, 128, 128], P('dp'), may hold values from -6 to 6
- slot_offset: int32 [384], P('dp'), may hold values from 0 to 5, as said below
- suffix_kv: bfloat16 [1024, 6, 2, 48, 128], P('dp'), may hold values from -7.1875 to 7.1875
- out_weight: bfloat16 [6144, 8192], P('mp'), may hold values from -0.078125 to 0.078125
Outputs:
- block_out: bfloat16 [1024, 8192], P('dp')
The draws below stay inside these ranges and needn't reach their ends.
Inputs may be any that keep to these rules, and one draw needn't show every extreme that they name: `slot_offset`: on every index of dp, among its 6 blocks no value occurs more than 2 times and some value occurs exactly 2 times. One document gets at most 12 blocks, and in every draw some document gets that many.
All inputs are finite; a program needn't handle non-finite values.
Results may differ from the reference program's by a relative error of at most 0.023.
Values may be sent and summed in bfloat16 or wider, within the bound.
A program may use at most 64 MiB of HBM per device.

```python
import jax
import jax.numpy as jnp
from jax import lax

D = 8192
HD = 128
GQA = 8
HEADS = 48
KV_HEADS = 6
SAMPLES = 16
SUFFIX = 48
BLK = 128
POOL_DEV = 6
SPREAD = 6
CAPACITY = 2
ROWS = 1024
POOL = 384
N_DP = 64


def pool_values(key):
    values = jax.random.normal(jax.random.fold_in(key, 11), (POOL, KV_HEADS, 2, BLK, HD), jnp.float32)
    values = jnp.clip(values, -6.0, 6.0)
    return values


def offset_lists(key):
    base_key = jax.random.fold_in(key, 5)
    device_keys = jax.random.split(base_key, N_DP)
    target = jax.random.randint(jax.random.fold_in(base_key, 1), (), 0, N_DP)
    device_ids = jnp.arange(N_DP, dtype=jnp.int32)
    forced = (target - device_ids) % N_DP

    def per_device(device_key, forced_lag):
        first_key, second_key, third_key = jax.random.split(device_key, 3)
        first_lag = jax.random.randint(first_key, (), 0, SPREAD)
        first_lag = jnp.where(forced_lag < SPREAD, forced_lag, first_lag).astype(jnp.int32)
        others = jax.random.permutation(second_key, jnp.arange((SPREAD - 1) * CAPACITY, dtype=jnp.int32) // CAPACITY)
        others = others + (others >= first_lag).astype(jnp.int32)
        listed = jnp.concatenate([jnp.zeros((CAPACITY,), jnp.int32) + first_lag, others[:POOL_DEV - CAPACITY]])
        return jax.random.permutation(third_key, listed)
    return jax.vmap(per_device)(device_keys, forced).reshape(-1).astype(jnp.int32)


def draw_prefix_pool(key, part):
    return pool_values(key).astype(jnp.bfloat16)


def draw_slot_offset(key, part):
    return offset_lists(key)


def draw_queries(key, part):
    base = 2.5 * jnp.clip(jax.random.normal(jax.random.fold_in(key, 3), (ROWS, HEADS * HD), jnp.float32), -6.0, 6.0)
    return base.astype(jnp.bfloat16)


def levels(stream_key, shape, cuts, smallest, largest):
    gain, own = 1.0, jax.random.fold_in(stream_key, 6)
    for axis_at, shards_of in cuts:
        heights = jnp.exp(jax.random.uniform(jax.random.fold_in(own, axis_at), (shards_of,), jnp.float32, smallest / len(cuts), largest / len(cuts)))
        gain = gain * jnp.repeat(heights, shape[axis_at] // shards_of).reshape([-1 if axis == axis_at else 1 for axis in range(len(shape))])
    return gain


def centred(own_key, dims, scale, reach, pieces=(), kind=jnp.bfloat16):
    values = jax.random.normal(own_key, dims, jnp.float32) * scale
    if len(pieces) > 0:
        values = levels(own_key, dims, pieces, -0.22, 0.18) * values
    return jnp.clip(values, min=-reach, max=reach).astype(kind)


def setup_inputs(seed: int = 0) -> dict:
    keys = jax.random.split(jax.random.key(seed), 6)
    return {
        "queries": draw_queries(jax.random.fold_in(keys[5], 71), 0),
        "prefix_pool": draw_prefix_pool(jax.random.fold_in(keys[5], 71), 0),
        "slot_offset": draw_slot_offset(jax.random.fold_in(keys[5], 71), 0),
        "suffix_kv": centred(keys[3], (ROWS, KV_HEADS, 2, SUFFIX, HD), 1.2, 7.1875, ((0, 64),)),
        "out_weight": centred(keys[4], (HEADS * HD, D), (HEADS * HD) ** -0.5, 0.078125, ((0, 12),)),
    }


NEG = -1.0e30


def rounded(values):
    return lax.optimization_barrier(values.astype(jnp.bfloat16)).astype(jnp.float32)


def reference(queries, prefix_pool, slot_offset, suffix_kv, out_weight):
    score_scale = HD ** -0.5
    lag_ids = jnp.arange(SPREAD, dtype=jnp.int32)
    slot_ids = jnp.arange(POOL_DEV, dtype=jnp.int32)

    def one_group(group):
        query_block = lax.dynamic_slice_in_dim(queries, group * SAMPLES, SAMPLES, 0).astype(jnp.float32)
        query_block = query_block.reshape(SAMPLES, KV_HEADS, GQA, HD)
        source = (group - lag_ids) % N_DP
        slot_list = (source[:, None] * POOL_DEV + slot_ids[None, :]).reshape(-1).astype(jnp.int32)
        live_slot = jnp.take(slot_offset, slot_list) == jnp.repeat(lag_ids, POOL_DEV)
        blocks = jnp.take(prefix_pool, slot_list, axis=0).astype(jnp.float32)
        key_rows = jnp.transpose(blocks[:, :, 0], (1, 0, 2, 3)).reshape(KV_HEADS, -1, HD)
        value_rows = jnp.transpose(blocks[:, :, 1], (1, 0, 2, 3)).reshape(KV_HEADS, -1, HD)
        live_rows = jnp.repeat(live_slot, BLK)
        prefix_scores = jnp.einsum("skgd,knd->skgn", query_block, key_rows) * score_scale
        prefix_scores = jnp.where(live_rows, prefix_scores, NEG)
        suffix_block = lax.dynamic_slice_in_dim(suffix_kv, group * SAMPLES, SAMPLES, 0).astype(jnp.float32)
        suffix_scores = jnp.einsum("skgd,sktd->skgt", query_block, suffix_block[:, :, 0]) * score_scale
        row_peak = jnp.maximum(prefix_scores.max(-1), suffix_scores.max(-1))
        prefix_weight = jnp.exp(prefix_scores - row_peak[..., None])
        suffix_weight = jnp.exp(suffix_scores - row_peak[..., None])
        denominator = prefix_weight.sum(-1) + suffix_weight.sum(-1)
        accumulated = jnp.einsum("skgn,knd->skgd", rounded(prefix_weight), value_rows)
        accumulated = accumulated + jnp.einsum("skgt,sktd->skgd", rounded(suffix_weight), suffix_block[:, :, 1])
        attended = (accumulated / denominator[..., None]).astype(jnp.bfloat16)
        return attended.reshape(SAMPLES, KV_HEADS * GQA * HD)

    attended = lax.map(one_group, jnp.arange(N_DP, dtype=jnp.int32))
    attended = attended.reshape(N_DP * SAMPLES, KV_HEADS * GQA * HD)
    return jnp.dot(attended, out_weight, preferred_element_type=jnp.float32).astype(jnp.bfloat16)
```

```python
import functools

import jax
import jax.numpy as jnp
from jax import lax
from jax.experimental import pallas as pl
from jax.experimental.pallas import tpu as pltpu
from jax.sharding import PartitionSpec as P

SPREAD = 6
GQA = 8
NEG = -1e30
NX = 4
NZ = 3
SPLITS = 2
MESH = pl.DeviceIdType.MESH
F32 = jnp.float32
BF16 = jnp.bfloat16


def dot_nt(a, b):
    return lax.dot_general(a, b, (((1,), (1,)), ((), ())), preferred_element_type=F32)


def dot_nn(a, b):
    return jnp.dot(a, b, preferred_element_type=F32)


def kernel(
    n_dp, q_ref, off_ref, pool_ref, suf_ref, w_ref, out_ref,
    kv, suf, w, vt, suft, qbuf, sacc, sst, racc, rst, psend, precv, own, zbuf,
    load_sem, w_sem, q_send, q_recv, a_send, a_recv, s_send, s_recv,
    p_send, p_recv, z_send, z_recv, g_send, g_recv,
):
    samples = q_ref.shape[0]
    local_heads = q_ref.shape[1] // 128
    rows = samples * local_heads
    n_blocks = pool_ref.shape[0]
    part = precv.shape[3]
    wide = SPLITS * part
    dp = lax.axis_index("dp")
    mp = lax.axis_index("mp")
    x = lax.rem(mp, NX)
    z = mp // NX
    head = mp * local_heads // GQA
    scale = 128 ** -0.5

    def dp_at(d):
        return lax.rem(dp + n_dp + d, n_dp)

    def x_at(d):
        return z * NX + lax.rem(x + d, NX)

    def z_at(d):
        return lax.rem(z + d, NZ) * NX + x

    pool_load = pltpu.make_async_copy(pool_ref.at[:, head], kv, load_sem.at[0])
    suf_load = pltpu.make_async_copy(suf_ref.at[:, head], suf, load_sem.at[1])
    pool_load.start()
    suf_load.start()

    barrier = pltpu.get_barrier_semaphore()
    for lag in range(1, SPREAD):
        for d in (lag, -lag):
            pl.semaphore_signal(barrier, inc=1, device_id={"dp": dp_at(d)}, device_id_type=MESH)
    for d in range(1, NX):
        pl.semaphore_signal(barrier, inc=1, device_id={"mp": x_at(d)}, device_id_type=MESH)
    for d in range(1, NZ):
        pl.semaphore_signal(barrier, inc=1, device_id={"mp": z_at(d)}, device_id_type=MESH)

    order = (2, 1, 3, 0)

    def columns(d, h):
        return pl.ds(pl.multiple_of(lax.rem(x + d, NX) * wide + h * part, part), part)

    w_loads = {}
    for h in range(SPLITS):
        for i, d in enumerate(order):
            w_loads[h, d] = pltpu.make_async_copy(
                w_ref.at[:, columns(d, h)], w.at[:, columns(d, h)], w_sem.at[h * NX + i]
            )
            w_loads[h, d].start()

    pl.semaphore_wait(barrier, 2 * (SPREAD - 1) + NX - 1 + NZ - 1)

    q_copies = []
    for lag in range(1, SPREAD):
        q_copies.append(
            pltpu.make_async_remote_copy(
                src_ref=q_ref, dst_ref=qbuf.at[lag - 1],
                send_sem=q_send.at[lag - 1], recv_sem=q_recv.at[lag - 1],
                device_id={"dp": dp_at(-lag)}, device_id_type=MESH,
            )
        )
    for copy in q_copies[::-1]:
        copy.start()

    low_lane = lax.broadcasted_iota(jnp.int32, (1, 128), 1) < rows

    def twice(q):
        pieces = [q[:, h * 128:(h + 1) * 128] for h in range(local_heads)]
        return jnp.concatenate(pieces + pieces, axis=0)

    def picked(lag):
        count, first, second = 0, 0, 0
        for b in range(n_blocks):
            hit = off_ref[b] == lag
            first = jnp.where(hit & (count == 0), b, first)
            second = jnp.where(hit & (count == 1), b, second)
            count = count + hit.astype(jnp.int32)
        return (
            (first, jnp.where(count >= 1, 0.0, NEG)),
            (second, jnp.where(count >= 2, 0.0, NEG)),
        )

    def block_scores(q2, picks):
        return [dot_nt(kv[b, 0], q2) * scale + bias for b, bias in picks]

    def packed(acc):
        return jnp.where(low_lane, acc[:rows], acc[rows:])

    pool_load.wait()
    for b in range(n_blocks):
        vt[b] = kv[b, 1].T
    suf_load.wait()
    suf_len = suf.shape[2]
    suf_keys = suf[:, 0].reshape(samples * suf_len, 128)
    suft[...] = suf[:, 1].reshape(samples * suf_len, 128).T

    q2 = twice(q_ref[...])
    picks = picked(0)
    scores = block_scores(q2, picks)
    owner = lax.broadcasted_iota(jnp.int32, (samples, suf_len, 128), 0).reshape(-1, 128)
    lane = lax.broadcasted_iota(jnp.int32, (samples * suf_len, 128), 1)
    suf_scores = jnp.where(owner == lax.rem(lane, samples), dot_nt(suf_keys, q2) * scale, NEG)
    peak0 = jnp.max(suf_scores, axis=0, keepdims=True)
    for s in scores:
        peak0 = jnp.maximum(peak0, jnp.max(s, axis=0, keepdims=True))
    weight = jnp.exp(suf_scores - peak0)
    total0 = jnp.sum(weight, axis=0, keepdims=True)
    acc = dot_nn(suft[...], weight.astype(BF16))
    for s, (b, _) in zip(scores, picks):
        weight = jnp.exp(s - peak0)
        total0 = total0 + jnp.sum(weight, axis=0, keepdims=True)
        acc = acc + dot_nn(vt[b], weight.astype(BF16))
    own_acc = packed(acc)

    back = []
    for lag in range(1, SPREAD):
        picks = picked(lag)
        q_copies[lag - 1].wait_recv()
        q2 = twice(qbuf[lag - 1])
        s1, s2 = block_scores(q2, picks)
        peak = jnp.maximum(
            jnp.max(s1, axis=0, keepdims=True), jnp.max(s2, axis=0, keepdims=True)
        )
        w1 = jnp.exp(s1 - peak)
        w2 = jnp.exp(s2 - peak)
        total = jnp.sum(w1, axis=0, keepdims=True) + jnp.sum(w2, axis=0, keepdims=True)
        acc = dot_nn(vt[picks[0][0]], w1.astype(BF16)) + dot_nn(vt[picks[1][0]], w2.astype(BF16))
        sacc[lag - 1] = packed(acc).astype(BF16)
        sst[lag - 1] = jnp.broadcast_to(jnp.where(low_lane, peak, total), (8, 128))
        for src, dst, send, recv in ((sacc, racc, a_send, a_recv), (sst, rst, s_send, s_recv)):
            copy = pltpu.make_async_remote_copy(
                src_ref=src.at[lag - 1], dst_ref=dst.at[lag - 1],
                send_sem=send.at[lag - 1], recv_sem=recv.at[lag - 1],
                device_id={"dp": dp_at(lag)}, device_id_type=MESH,
            )
            copy.start()
            back.append(copy)

    for copy in back:
        copy.wait_recv()
    peaks, totals = [peak0], [total0]
    for lag in range(1, SPREAD):
        st = rst[lag - 1]
        turned = pltpu.roll(st, rows, 1)
        peaks.append(jnp.where(low_lane, st, turned)[0:1])
        totals.append(jnp.where(low_lane, turned, st)[0:1])
    peak = functools.reduce(jnp.maximum, peaks)
    factors = [jnp.exp(p - peak) for p in peaks]
    total = factors[0] * total0
    acc = factors[0] * own_acc
    for lag in range(1, SPREAD):
        total = total + factors[lag] * totals[lag]
        acc = acc + factors[lag] * racc[lag - 1].astype(F32)
    acc = acc / total
    acc = jnp.concatenate([acc, pltpu.roll(acc, rows, 1)], axis=0).T
    attended = jnp.concatenate(
        [acc[h * samples:(h + 1) * samples] for h in range(local_heads)], axis=1
    ).astype(BF16)

    p_copies = {}
    for h in range(SPLITS):
        for d in order:
            w_loads[h, d].wait()
            product = dot_nn(attended, w[:, columns(d, h)])
            if d == 0:
                own[h] = product
            else:
                psend[d - 1, h] = product.astype(BF16)
                p_copies[h, d] = pltpu.make_async_remote_copy(
                    src_ref=psend.at[d - 1, h], dst_ref=precv.at[d - 1, h],
                    send_sem=p_send.at[d - 1, h], recv_sem=p_recv.at[d - 1, h],
                    device_id={"mp": x_at(d)}, device_id_type=MESH,
                )
                p_copies[h, d].start()

    z_copies = {}
    for h in range(SPLITS):
        value = own[h]
        for d in range(1, NX):
            p_copies[h, d].wait_recv()
            value = value + precv[d - 1, h].astype(F32)
        zbuf[z, h] = value.astype(BF16)
        for d in range(1, NZ):
            z_copies[h, d] = pltpu.make_async_remote_copy(
                src_ref=zbuf.at[z, h], dst_ref=zbuf.at[z, h],
                send_sem=z_send.at[d - 1, h], recv_sem=z_recv.at[d - 1, h],
                device_id={"mp": z_at(d)}, device_id_type=MESH,
            )
            z_copies[h, d].start()

    g_copies = {}
    for h in range(SPLITS):
        for d in range(1, NZ):
            z_copies[h, d].wait_recv()
        value = zbuf[0, h].astype(F32) + zbuf[1, h].astype(F32) + zbuf[2, h].astype(F32)
        out_ref[:, columns(0, h)] = value.astype(BF16)
        for d in range(1, NX):
            g_copies[h, d] = pltpu.make_async_remote_copy(
                src_ref=out_ref.at[:, columns(0, h)], dst_ref=out_ref.at[:, columns(0, h)],
                send_sem=g_send.at[d - 1, h], recv_sem=g_recv.at[d - 1, h],
                device_id={"mp": x_at(d)}, device_id_type=MESH,
            )
            g_copies[h, d].start()

    for h in range(SPLITS):
        for d in range(1, NX):
            g_copies[h, d].wait_recv()
    for copy in (*q_copies, *back, *p_copies.values(), *z_copies.values(), *g_copies.values()):
        copy.wait_send()


def local(n_dp, queries, prefix_pool, slot_offset, suffix_kv, out_weight):
    samples, width = queries.shape
    n_blocks, _, _, blk, hd = prefix_pool.shape
    depth, wide = out_weight.shape
    part = wide // (NX * SPLITS)
    suf_len = suffix_kv.shape[3]
    lags = SPREAD - 1
    rows = samples * width // hd
    dma = pltpu.SemaphoreType.DMA
    any_space = pl.BlockSpec(memory_space=pl.ANY)
    return pl.pallas_call(
        functools.partial(kernel, n_dp),
        out_shape=jax.ShapeDtypeStruct((samples, wide), BF16),
        in_specs=[
            pl.BlockSpec(memory_space=pltpu.VMEM),
            pl.BlockSpec(memory_space=pltpu.SMEM),
            any_space,
            any_space,
            any_space,
        ],
        out_specs=pl.BlockSpec(memory_space=pltpu.VMEM),
        scratch_shapes=[
            pltpu.VMEM((n_blocks, 2, blk, hd), BF16),
            pltpu.VMEM((samples, 2, suf_len, hd), BF16),
            pltpu.VMEM((depth, wide), BF16),
            pltpu.VMEM((n_blocks, hd, blk), BF16),
            pltpu.VMEM((hd, samples * suf_len), BF16),
            pltpu.VMEM((lags, samples, width), BF16),
            pltpu.VMEM((lags, rows, hd), BF16),
            pltpu.VMEM((lags, 8, hd), F32),
            pltpu.VMEM((lags, rows, hd), BF16),
            pltpu.VMEM((lags, 8, hd), F32),
            pltpu.VMEM((NX - 1, SPLITS, samples, part), BF16),
            pltpu.VMEM((NX - 1, SPLITS, samples, part), BF16),
            pltpu.VMEM((SPLITS, samples, part), F32),
            pltpu.VMEM((NZ, SPLITS, samples, part), BF16),
            dma((2,)),
            dma((NX * SPLITS,)),
            dma((lags,)),
            dma((lags,)),
            dma((lags,)),
            dma((lags,)),
            dma((lags,)),
            dma((lags,)),
            dma((NX - 1, SPLITS)),
            dma((NX - 1, SPLITS)),
            dma((NZ - 1, SPLITS)),
            dma((NZ - 1, SPLITS)),
            dma((NX - 1, SPLITS)),
            dma((NX - 1, SPLITS)),
        ],
        compiler_params=pltpu.CompilerParams(collective_id=0, has_side_effects=True),
    )(queries, slot_offset, prefix_pool, suffix_kv, out_weight)


def solution(mesh):
    placed = (
        P("dp", "mp"),
        P("dp", None, None, None, None),
        P("dp"),
        P("dp", None, None, None, None),
        P("mp", None),
    )
    return jax.shard_map(
        functools.partial(local, mesh.shape["dp"]),
        mesh=mesh, in_specs=placed, out_specs=P("dp", None), check_vma=False,
    )
```

```python
import functools

import jax
import jax.numpy as jnp
from jax import lax
from jax.experimental import pallas as pl
from jax.experimental.pallas import tpu as pltpu
from jax.sharding import PartitionSpec as P

SPREAD = 6
GQA = 8
NEG = -1e30
NX = 4
NZ = 3
LANES = 128
MESH = pl.DeviceIdType.MESH
F32 = jnp.float32
BF16 = jnp.bfloat16


def dot_nt(a, b):
    return lax.dot_general(a, b, (((1,), (1,)), ((), ())), preferred_element_type=F32)


def dot_nn(a, b):
    return jnp.dot(a, b, preferred_element_type=F32)


def kernel(
    n_dp, q_hbm, off_hbm, pool_ref, suf_ref, w_ref, out_ref,
    q_ref, off_ref, kv, suf, w, vt, suft, qbuf, sacc, sst, racc, rst, psend, precv, gbuf,
    load_sem, w_sem, q_send, q_recv, a_send, a_recv, s_send, s_recv,
    p_send, p_recv, g_send, g_recv,
):
    samples = q_hbm.shape[0]
    local_heads = q_hbm.shape[1] // 128
    rows = samples * local_heads
    n_blocks = pool_ref.shape[0]
    part = precv.shape[2]
    wide = out_ref.shape[1] // NX
    step = (wide // LANES) // NZ * LANES
    dp = lax.axis_index("dp")
    mp = lax.axis_index("mp")
    x = lax.rem(mp, NX)
    z = mp // NX
    head = mp * local_heads // GQA
    scale = 128 ** -0.5

    def dp_at(d):
        return lax.rem(dp + n_dp + d, n_dp)

    def peer(dz, dx):
        return lax.rem(z + dz, NZ), lax.rem(x + dx, NX)

    def mp_at(dz, dx):
        pz, px = peer(dz, dx)
        return pz * NX + px

    others = [(dz, dx) for dx in (2, 1, 3, 0) for dz in range(NZ) if (dz, dx) != (0, 0)]

    barrier = pltpu.get_barrier_semaphore()
    for lag in range(1, SPREAD):
        for d in (lag, -lag):
            pl.semaphore_signal(barrier, inc=1, device_id={"dp": dp_at(d)}, device_id_type=MESH)
    for dz, dx in others:
        pl.semaphore_signal(barrier, inc=1, device_id={"mp": mp_at(dz, dx)}, device_id_type=MESH)

    pool_load = pltpu.make_async_copy(pool_ref.at[:, head], kv, load_sem.at[0])
    suf_load = pltpu.make_async_copy(suf_ref.at[:, head], suf, load_sem.at[1])
    q_load = pltpu.make_async_copy(q_hbm, q_ref, load_sem.at[2])
    off_load = pltpu.make_async_copy(off_hbm, off_ref, load_sem.at[3])
    q_load.start()
    off_load.start()
    pool_load.start()
    suf_load.start()

    w_loads = []
    for i in range(NX):
        cols = pl.ds(i * wide, wide)
        w_loads.append(pltpu.make_async_copy(w_ref.at[:, cols], w.at[:, cols], w_sem.at[i]))
        w_loads[i].start()

    pl.semaphore_wait(barrier, 2 * (SPREAD - 1) + len(others))

    q_copies = []
    for lag in range(1, SPREAD):
        q_copies.append(
            pltpu.make_async_remote_copy(
                src_ref=q_hbm, dst_ref=qbuf.at[lag - 1],
                send_sem=q_send.at[lag - 1], recv_sem=q_recv.at[lag - 1],
                device_id={"dp": dp_at(-lag)}, device_id_type=MESH,
            )
        )
    for copy in q_copies[::-1]:
        copy.start()

    low_lane = lax.broadcasted_iota(jnp.int32, (1, 128), 1) < rows

    def twice(q):
        pieces = [q[:, h * 128:(h + 1) * 128] for h in range(local_heads)]
        return jnp.concatenate(pieces + pieces, axis=0)

    def picked(lag):
        count, first, second = 0, 0, 0
        for b in range(n_blocks):
            hit = off_ref[b] == lag
            first = jnp.where(hit & (count == 0), b, first)
            second = jnp.where(hit & (count == 1), b, second)
            count = count + hit.astype(jnp.int32)
        return (
            (first, jnp.where(count >= 1, 0.0, NEG)),
            (second, jnp.where(count >= 2, 0.0, NEG)),
        )

    def block_scores(q2, picks):
        return [dot_nt(kv[b, 0], q2) * scale + bias for b, bias in picks]

    def packed(acc):
        return jnp.where(low_lane, acc[:rows], acc[rows:])

    off_load.wait()
    q_load.wait()
    pool_load.wait()
    for b in range(n_blocks):
        vt[b] = kv[b, 1].T
    suf_load.wait()
    suf_len = suf.shape[2]
    suf_keys = suf[:, 0].reshape(samples * suf_len, 128)
    suft[...] = suf[:, 1].reshape(samples * suf_len, 128).T

    q2 = twice(q_ref[...])
    picks = picked(0)
    scores = block_scores(q2, picks)
    owner = lax.broadcasted_iota(jnp.int32, (samples, suf_len, 128), 0).reshape(-1, 128)
    lane = lax.broadcasted_iota(jnp.int32, (samples * suf_len, 128), 1)
    suf_scores = jnp.where(owner == lax.rem(lane, samples), dot_nt(suf_keys, q2) * scale, NEG)
    peak0 = jnp.max(suf_scores, axis=0, keepdims=True)
    for s in scores:
        peak0 = jnp.maximum(peak0, jnp.max(s, axis=0, keepdims=True))
    weight = jnp.exp(suf_scores - peak0)
    total0 = jnp.sum(weight, axis=0, keepdims=True)
    acc = dot_nn(suft[...], weight.astype(BF16))
    for s, (b, _) in zip(scores, picks):
        weight = jnp.exp(s - peak0)
        total0 = total0 + jnp.sum(weight, axis=0, keepdims=True)
        acc = acc + dot_nn(vt[b], weight.astype(BF16))
    own_acc = packed(acc)

    back = []
    for lag in range(1, SPREAD):
        picks = picked(lag)
        q_copies[lag - 1].wait_recv()
        q2 = twice(qbuf[lag - 1])
        s1, s2 = block_scores(q2, picks)
        peak = jnp.maximum(
            jnp.max(s1, axis=0, keepdims=True), jnp.max(s2, axis=0, keepdims=True)
        )
        w1 = jnp.exp(s1 - peak)
        w2 = jnp.exp(s2 - peak)
        total = jnp.sum(w1, axis=0, keepdims=True) + jnp.sum(w2, axis=0, keepdims=True)
        acc = dot_nn(vt[picks[0][0]], w1.astype(BF16)) + dot_nn(vt[picks[1][0]], w2.astype(BF16))
        sacc[lag - 1] = packed(acc).astype(BF16)
        sst[lag - 1] = jnp.where(low_lane, peak, total)
        for src, dst, send, recv in ((sacc, racc, a_send, a_recv), (sst, rst, s_send, s_recv)):
            copy = pltpu.make_async_remote_copy(
                src_ref=src.at[lag - 1], dst_ref=dst.at[lag - 1],
                send_sem=send.at[lag - 1], recv_sem=recv.at[lag - 1],
                device_id={"dp": dp_at(lag)}, device_id_type=MESH,
            )
            copy.start()
            back.append(copy)

    for copy in back:
        copy.wait_recv()
    peaks, totals = [peak0], [total0]
    for lag in range(1, SPREAD):
        st = rst[lag - 1]
        turned = pltpu.roll(st, rows, 1)
        peaks.append(jnp.where(low_lane, st, turned))
        totals.append(jnp.where(low_lane, turned, st))
    peak = functools.reduce(jnp.maximum, peaks)
    factors = [jnp.exp(p - peak) for p in peaks]
    total = factors[0] * total0
    acc = factors[0] * own_acc
    for lag in range(1, SPREAD):
        total = total + factors[lag] * totals[lag]
        acc = acc + factors[lag] * racc[lag - 1].astype(F32)
    acc = acc / total
    acc = jnp.concatenate([acc, pltpu.roll(acc, rows, 1)], axis=0).T
    attended = jnp.concatenate(
        [acc[h * samples:(h + 1) * samples] for h in range(local_heads)], axis=1
    ).astype(BF16)

    def product(dz, dx):
        pz, px = peer(dz, dx)
        start = pl.multiple_of(px * wide + pz * step, LANES)
        return dot_nn(attended, w[:, pl.ds(start, part)])

    for load in w_loads:
        load.wait()
    p_copies = []
    for i, (dz, dx) in enumerate(others):
        psend[i] = product(dz, dx).astype(BF16)
        copy = pltpu.make_async_remote_copy(
            src_ref=psend.at[i], dst_ref=precv.at[i],
            send_sem=p_send.at[i], recv_sem=p_recv.at[i],
            device_id={"mp": mp_at(dz, dx)}, device_id_type=MESH,
        )
        copy.start()
        p_copies.append(copy)
    value = product(0, 0)
    for i in reversed(range(len(others))):
        p_copies[i].wait_recv()
        value = value + precv[i].astype(F32)
    gbuf[mp] = value.astype(BF16)

    g_copies = []
    for i, (dz, dx) in enumerate(others):
        copy = pltpu.make_async_remote_copy(
            src_ref=gbuf.at[mp], dst_ref=gbuf.at[mp],
            send_sem=g_send.at[i], recv_sem=g_recv.at[i],
            device_id={"mp": mp_at(dz, dx)}, device_id_type=MESH,
        )
        copy.start()
        g_copies.append(copy)
    for copy in g_copies:
        copy.wait_recv()
    for pz in range(NZ):
        count = part if pz == NZ - 1 else step
        for px in range(NX):
            start = px * wide + pz * step
            out_ref[:, start:start + count] = gbuf[pz * NX + px, :, 0:count]
    for copy in (*q_copies, *back, *p_copies, *g_copies):
        copy.wait_send()


def local(n_dp, queries, prefix_pool, slot_offset, suffix_kv, out_weight):
    samples, width = queries.shape
    n_blocks, _, _, blk, hd = prefix_pool.shape
    depth, wide = out_weight.shape
    tiles = wide // (NX * LANES)
    part = (tiles - (NZ - 1) * (tiles // NZ)) * LANES
    peers = NX * NZ - 1
    suf_len = suffix_kv.shape[3]
    lags = SPREAD - 1
    rows = samples * width // hd
    dma = pltpu.SemaphoreType.DMA
    any_space = pl.BlockSpec(memory_space=pl.ANY)
    return pl.pallas_call(
        functools.partial(kernel, n_dp),
        out_shape=pltpu.VMEM((samples, wide), BF16),
        in_specs=[
            any_space,
            any_space,
            any_space,
            any_space,
            any_space,
        ],
        out_specs=pl.BlockSpec(memory_space=pltpu.VMEM),
        scratch_shapes=[
            pltpu.VMEM((samples, width), BF16),
            pltpu.SMEM((n_blocks,), jnp.int32),
            pltpu.VMEM((n_blocks, 2, blk, hd), BF16),
            pltpu.VMEM((samples, 2, suf_len, hd), BF16),
            pltpu.VMEM((depth, wide), BF16),
            pltpu.VMEM((n_blocks, hd, blk), BF16),
            pltpu.VMEM((hd, samples * suf_len), BF16),
            pltpu.VMEM((lags, samples, width), BF16),
            pltpu.VMEM((lags, rows, hd), BF16),
            pltpu.VMEM((lags, 1, hd), F32),
            pltpu.VMEM((lags, rows, hd), BF16),
            pltpu.VMEM((lags, 1, hd), F32),
            pltpu.VMEM((peers, samples, part), BF16),
            pltpu.VMEM((peers, samples, part), BF16),
            pltpu.VMEM((NX * NZ, samples, part), BF16),
            dma((4,)),
            dma((NX,)),
            dma((lags,)),
            dma((lags,)),
            dma((lags,)),
            dma((lags,)),
            dma((lags,)),
            dma((lags,)),
            dma((peers,)),
            dma((peers,)),
            dma((peers,)),
            dma((peers,)),
        ],
        compiler_params=pltpu.CompilerParams(collective_id=0, has_side_effects=True),
    )(queries, slot_offset, prefix_pool, suffix_kv, out_weight)


def solution(mesh):
    placed = (
        P("dp", "mp"),
        P("dp", None, None, None, None),
        P("dp"),
        P("dp", None, None, None, None),
        P("mp", None),
    )
    return jax.shard_map(
        functools.partial(local, mesh.shape["dp"]),
        mesh=mesh, in_specs=placed, out_specs=P("dp", None), check_vma=False,
    )
```
